256 devices in a mesh: section: 64 (over z_hi, y, x, core), tp: 4 (over z_lo).
Axes of the slice: x: 4, y: 4, z: 8 (z_hi: 2, z_lo: 4; z = z_hi * 4 + z_lo), core: 2. Of those that a mesh axis runs over, the one named last changes fastest.
Arguments:
- param: float32 [4096, 3584], P('section', 'tp'), may hold values from -4 to 4
- moment_one: float32 [4096, 3584], P('section', 'tp'), may hold values from -2 to 2
- moment_two: float32 [4096, 3584], P('section', 'tp'), may hold values from 0.001 to 1
- proj_grad: float32 [4096, 3584], P('section', 'tp'), may hold values from -6 to 6
- embed_grad: bfloat16 [32768, 3584], P('section', 'tp'), may hold values from -6 to 6
- token_ids: int32 [32768], P('section'), may hold values from 0 to 4095, as said below
- next_ids: int32 [32768], P('section'), may hold values from 0 to 4095, as said below
Outputs:
- new_param: float32 [4096, 3584], P('section', 'tp')
- new_moment_one: float32 [4096, 3584], P('section', 'tp')
- new_moment_two: float32 [4096, 3584], P('section', 'tp')
- next_rows: bfloat16 [32768, 3584], P('section')
The draws below stay inside these ranges and needn't reach their ends.
Inputs may be any that keep to these rules, and one draw needn't show every extreme that they name: `token_ids`: in each section index's block of 512 tokens at most 16 ids fall into any one owner's run of 64 table rows (id // 64); in every draw some owner receives exactly 16 from every block. `next_ids`: the same bound of 16 a block and an owner holds, and is reached, as for token_ids.
All inputs are finite; a program needn't handle non-finite values.
Results may differ from the reference program's by a relative error of at most 0.001.
Values may be sent and summed in bfloat16 or wider, within the bound.
No kernel may reach another device: no remote copies, remote signals or barrier semaphores. Data moves between devices by JAX's collectives and lax.ppermute only.
A program may use at most 64 MiB of HBM per device.

```python
import math
import jax
import jax.numpy as jnp

D = 3584
ROWS_OWN = 64
TOK_DEV = 512
STEP = 1000
VOCAB = 4096
TOKENS = 32768
CAP = 16


def owner_ids(key, salt):
    key = jax.random.fold_in(key, salt)
    blocks = TOKENS // TOK_DEV
    owners = VOCAB // ROWS_OWN
    slots = owners * CAP
    key_common, key_own, key_score, key_rows, key_order = jax.random.split(key, 5)
    common = jax.random.randint(key_common, (), 0, owners)
    single = jax.random.randint(key_own, (blocks,), 0, owners - 1)
    single = single + (single >= common).astype(jnp.int32)
    scores = jax.random.randint(key_score, (blocks, slots), 0, 2 ** 16) * slots + jnp.arange(slots)[None, :]
    slot_owner = jnp.arange(slots) // CAP
    forced = (slot_owner[None, :] == common) | (slot_owner[None, :] == single[:, None])
    scores = jnp.where(forced, scores - 2 ** 28, scores)
    picked = jnp.argsort(scores, axis=1, stable=True)[:, :TOK_DEV]
    owner = picked // CAP
    mixing = jax.random.randint(key_order, (blocks, TOK_DEV), 0, 2 ** 16) * TOK_DEV + jnp.arange(TOK_DEV)[None, :]
    order = jnp.argsort(mixing, axis=1, stable=True)
    owner = jnp.take_along_axis(owner, order, axis=1)
    within = jax.random.randint(key_rows, (blocks, TOK_DEV), 0, ROWS_OWN)
    return (owner * ROWS_OWN + within).reshape(-1).astype(jnp.int32)


def draw_token_ids(key, part):
    return owner_ids(key, 11)


def draw_next_ids(key, part):
    return owner_ids(key, 23)


def steps_of(own_key, extent, pieces, smallest, largest):
    def one(position, parts):
        draws = jax.random.uniform(jax.random.fold_in(jax.random.fold_in(own_key, 6), position), (parts,), jnp.float32, smallest / len(pieces), largest / len(pieces))
        return jnp.repeat(jnp.exp(draws), extent[position] // parts).reshape((-1,) + (1,) * (len(extent) - position - 1))

    loudness = one(*pieces[0])
    for cut in pieces[1:]:
        loudness = loudness * one(*cut)
    return loudness


def gaussian(key, dims, width, reach, shards=(), held_as=jnp.bfloat16):
    factor_of = steps_of(key, dims, shards, -0.22, 0.18) if shards else 1.0
    result = jax.random.normal(key, dims, jnp.float32) * width * factor_of
    return jnp.minimum(jnp.maximum(result, -reach), reach).astype(held_as)


def setup_inputs(seed: int = 0) -> dict:
    key_list = jax.random.split(jax.random.key(seed), 8)
    return {
        "param": gaussian(key_list[0], (VOCAB, D), 0.5, 4.0, ((0, 64), (1, 4)), jnp.float32),
        "moment_one": gaussian(key_list[1], (VOCAB, D), 0.2, 2.0, ((0, 64), (1, 4)), jnp.float32),
        "moment_two": jnp.clip(jnp.exp(math.log(1.0) - 6.9077552 * jax.random.uniform(key_list[2], (VOCAB, D), jnp.float32) ** steps_of(key_list[2], (VOCAB, D), ((0, 64), (1, 4)), -0.2, 0.2)), 0.001, 1.0),
        "proj_grad": gaussian(key_list[3], (VOCAB, D), 1.0, 6.0, ((0, 64), (1, 4)), jnp.float32),
        "embed_grad": gaussian(key_list[4], (TOKENS, D), 1.0, 6.0, ((0, 64), (1, 4))),
        "token_ids": draw_token_ids(jax.random.fold_in(key_list[7], 71), 0),
        "next_ids": draw_next_ids(jax.random.fold_in(key_list[7], 71), 0),
    }


def reference(param, moment_one, moment_two, proj_grad, embed_grad, token_ids, next_ids):
    embed_sum = jnp.zeros((VOCAB, D), jnp.float32).at[token_ids].add(embed_grad.astype(jnp.float32))
    grad = proj_grad + embed_sum
    new_moment_one = 0.9 * moment_one + 0.1 * grad
    new_moment_two = 0.999 * moment_two + 0.001 * grad * grad
    first_fix = 1.0 - 0.9 ** STEP
    second_fix = 1.0 - 0.999 ** STEP
    new_param = param - 0.01 * (new_moment_one / first_fix) / (jnp.sqrt(new_moment_two / second_fix) + 1e-08)
    table = new_param.astype(jnp.bfloat16)
    next_rows = jnp.take(table, next_ids, axis=0)
    return (new_param, new_moment_one, new_moment_two, next_rows)
```

```python
import functools

import jax
import jax.numpy as jnp
from jax import lax
from jax.experimental import pallas as pl
from jax.experimental.pallas import tpu as pltpu
from jax.sharding import Mesh, PartitionSpec as P

STEP = 1000
PLANE = ("y", "x", "c")
SECTION = ("zh",) + PLANE
PAIR = [(0, 1), (1, 0)]
LANES = 128
VMEM = pl.BlockSpec(memory_space=pltpu.VMEM)
SMEM = pl.BlockSpec(memory_space=pltpu.SMEM)
ANY = pl.BlockSpec(memory_space=pl.ANY)
BF16, F32, I32 = jnp.bfloat16, jnp.float32, jnp.int32


def iota(shape, dim):
    return lax.broadcasted_iota(I32, shape, dim)


def call(body, out, n_in, specs=None, out_specs=None, cost=(0, 0), scratch=(), name=None, vmem=20):
    return pl.pallas_call(
        body,
        out_shape=out,
        in_specs=specs or [VMEM] * n_in,
        out_specs=out_specs or jax.tree.map(lambda _: VMEM, out),
        scratch_shapes=scratch,
        name=name,
        compiler_params=pltpu.CompilerParams(vmem_limit_bytes=vmem << 20),
        cost_estimate=pl.CostEstimate(flops=cost[0], bytes_accessed=cost[1], transcendentals=0),
    )


def split_ids(ids, rows_own, places):
    owner = ids // rows_own
    return owner % places, ids + (owner // places - owner) * rows_own


def slots_of_row(ids, rows_own, places, per_place):
    tokens = ids.shape[1]
    place, local = split_ids(ids, rows_own, places)
    hits = iota((places, tokens), 0) == place
    earlier = (iota((tokens, tokens), 0) < iota((tokens, tokens), 1)).astype(BF16)
    before = jnp.dot(hits.astype(BF16), earlier, preferred_element_type=F32)
    rank = jnp.sum(jnp.where(hits, before, 0.0), axis=0, keepdims=True).astype(I32)
    return place * per_place + rank, local


def pack_body(places, rows_own, token_ref, next_ref, grad_ref, out_ref):
    tokens, width = grad_ref.shape
    slots = out_ref.shape[0]
    per_place = slots // places
    tags = jnp.zeros((slots, LANES), F32)
    for lane, ids_ref in enumerate((token_ref, next_ref)):
        slot, local = slots_of_row(ids_ref[...], rows_own, places, per_place)
        chosen = (iota((slots, tokens), 0) == slot).astype(BF16)
        if lane == 0:
            out_ref[:, :width] = jnp.dot(chosen, grad_ref[...], preferred_element_type=F32).astype(BF16)
        marks = jnp.where(iota((LANES, tokens), 0) == lane, local + 1, 0).astype(F32).astype(BF16)
        tags += lax.dot_general(chosen, marks, (((1,), (1,)), ((), ())), preferred_element_type=F32)
    out_ref[:, width:] = tags.astype(BF16)


def chosen_rows(got_ref, lane, width, rows, half_ref):
    tag = got_ref[:, width + lane : width + lane + 1].astype(F32).astype(I32) - 1
    row = iota((got_ref.shape[0], rows), 1)
    half = rows // 2
    mine_first = jnp.where(row < half, row + half_ref[0] * half, row - half_ref[0] * half)
    return (tag == mine_first).astype(F32).astype(BF16)


def sum_body(half_ref, got_ref, mine_ref, other_ref):
    half, width = mine_ref.shape
    chosen = chosen_rows(got_ref, 0, width, 2 * half, half_ref)
    total = lax.dot_general(
        chosen, got_ref[:, :width], (((0,), (0,)), ((), ())), preferred_element_type=F32
    )
    mine_ref[...] = total[:half]
    other_ref[...] = total[half:]


def ask_body(half_ref, got_ref, out_ref):
    out_ref[...] = chosen_rows(got_ref, 1, got_ref.shape[1] - LANES, out_ref.shape[1], half_ref)


def adam_body(param_ref, one_ref, two_ref, proj_ref, mine_ref, other_ref, p_ref, o_ref, t_ref, table_ref):
    grad = proj_ref[...] + (mine_ref[...] + other_ref[...])
    one = 0.9 * one_ref[...] + 0.1 * grad
    two = 0.999 * two_ref[...] + 0.001 * grad * grad
    first_fix = 1.0 - 0.9**STEP
    second_fix = 1.0 - 0.999**STEP
    param = param_ref[...] - 0.01 * (one / first_fix) / (jnp.sqrt(two / second_fix) + 1e-08)
    o_ref[...] = one
    t_ref[...] = two
    p_ref[...] = param
    table_ref[...] = param.astype(BF16)


def find_body(chosen_ref, mine_ref, other_ref, out_ref):
    half = mine_ref.shape[0]
    found = jnp.dot(chosen_ref[:, :half], mine_ref[...], preferred_element_type=F32)
    found += jnp.dot(chosen_ref[:, half:], other_ref[...], preferred_element_type=F32)
    out_ref[...] = found.astype(BF16)


def route_body(places, rows_own, ids_ref, out_ref):
    tokens, slots = out_ref.shape
    place, _ = split_ids(ids_ref[...], rows_own, places)
    hits = iota((tokens, LANES), 1) == place
    earlier = (iota((tokens, tokens), 1) < iota((tokens, tokens), 0)).astype(BF16)
    before = jnp.dot(earlier, hits.astype(BF16), preferred_element_type=F32)
    rank = jnp.sum(jnp.where(hits, before, 0.0), axis=1, keepdims=True).astype(I32)
    slot = place * (slots // places) + rank
    out_ref[...] = (iota((tokens, slots), 1) == slot).astype(BF16)


def pick_body(route_ref, replies_ref, out_ref):
    out_ref[...] = jnp.dot(route_ref[...], replies_ref[...], preferred_element_type=F32).astype(BF16)


def join_body(ranks, me_ref, own_ref, *refs):
    ups, downs = refs[: ranks - 1], refs[ranks - 1 : 2 * ranks - 2]
    out_ref, sems = refs[-2:]
    me = me_ref[0]
    width = own_ref.shape[1]

    def copy(src, rank, sem):
        columns = pl.ds(pl.multiple_of(rank * width, LANES), width)
        return pltpu.make_async_copy(src, out_ref.at[:, columns], sems.at[sem])

    copies = [(None, copy(own_ref, me, 0))]
    for k in range(1, ranks):
        copies.append((me >= k, copy(ups[k - 1], jnp.maximum(me - k, 0), k)))
        copies.append((me + k < ranks, copy(downs[k - 1], jnp.minimum(me + k, ranks - 1), ranks - 1 + k)))
    for cond, c in copies:
        if cond is None:
            c.start()
        else:
            pl.when(cond)(c.start)
    for cond, c in copies:
        if cond is None:
            c.wait()
        else:
            pl.when(cond)(c.wait)


def on_device(param, moment_one, moment_two, proj_grad, embed_grad, token_ids, next_ids):
    rows_own, width = param.shape
    places = lax.axis_size(PLANE)
    ranks = lax.axis_size("tp")
    tokens = token_ids.shape[0]
    slots = 2 * tokens
    sds = jax.ShapeDtypeStruct
    half = lax.axis_index("zh").reshape(1)
    me = lax.axis_index("tp").reshape(1)

    packed = call(
        functools.partial(pack_body, places, rows_own), sds((slots, width + LANES), BF16), 3,
        cost=(2 * slots * tokens * width, 4 << 20), name="pack",
    )(token_ids.reshape(1, -1), next_ids.reshape(1, -1), embed_grad)
    got = lax.all_to_all(
        packed.reshape(places, slots // places, width + LANES), PLANE, split_axis=0, concat_axis=0, tiled=True
    ).reshape(slots, width + LANES)
    route = call(
        functools.partial(route_body, places, rows_own), sds((tokens, slots), BF16), 1,
        cost=(2 * tokens * tokens * LANES, 2 << 20), name="route",
    )(next_ids.reshape(-1, 1))
    mine, other = call(
        sum_body, (sds((rows_own, width), F32),) * 2, 2, specs=[SMEM, VMEM],
        cost=(4 * slots * rows_own * width, 3 << 20), name="sum",
    )(half, got)
    theirs = lax.ppermute(other, "zh", PAIR)
    chosen = call(
        ask_body, sds((slots, 2 * rows_own), BF16), 2, specs=[SMEM, VMEM],
        cost=(slots * LANES, 1 << 20), name="ask",
    )(half, got)
    block = sds((rows_own, width), F32)
    new_param, new_one, new_two, table = call(
        adam_body, (block, block, block, sds((rows_own, width), BF16)), 6,
        cost=(20 * rows_own * width, 2 << 20), name="adam",
    )(param, moment_one, moment_two, proj_grad, mine, theirs)
    table_other = lax.ppermute(table, "zh", PAIR)
    found = call(
        find_body, sds((slots, width), BF16), 3, cost=(4 * slots * rows_own * width, 3 << 20), name="find",
    )(chosen, table, table_other)
    replies = lax.all_to_all(
        found.reshape(places, slots // places, width), PLANE, split_axis=0, concat_axis=0, tiled=True
    ).reshape(slots, width)
    own = call(
        pick_body, sds((tokens, width), BF16), 2, cost=(2 * slots * tokens * width, 4 << 20), name="pick",
    )(route, replies)
    ups, downs = [], []
    up = down = own
    for k in range(1, ranks):
        up = lax.ppermute(up, "tp", [(i, i + 1) for i in range(k - 1, ranks - 1)])
        down = lax.ppermute(down, "tp", [(i, i - 1) for i in range(1, ranks - k + 1)])
        ups.append(up)
        downs.append(down)
    next_rows = call(
        functools.partial(join_body, ranks), sds((tokens, ranks * width), BF16), 0,
        specs=[SMEM] + [ANY] * (2 * ranks - 1), out_specs=ANY,
        scratch=[pltpu.SemaphoreType.DMA((2 * ranks - 1,))],
        cost=(0, 8 << 20), name="join",
    )(me, own, *ups, *downs)
    return (new_param, new_one, new_two, next_rows)


def solution(mesh):
    grid = Mesh(mesh.devices.reshape(2, 4, 4, 2, mesh.shape["tp"]), SECTION + ("tp",))
    block = P(SECTION, "tp")
    return jax.shard_map(
        on_device,
        mesh=grid,
        in_specs=(block,) * 5 + (P(SECTION),) * 2,
        out_specs=(block,) * 3 + (P(SECTION, None),),
        check_vma=False,
    )
```

```python
import functools

import jax
import jax.numpy as jnp
from jax import lax
from jax.experimental import pallas as pl
from jax.experimental.pallas import tpu as pltpu
from jax.sharding import Mesh, PartitionSpec as P

STEP = 1000
PLANE = ("y", "x", "c")
SECTION = ("zh",) + PLANE
PAIR = [(0, 1), (1, 0)]
LANES = 128
VMEM = pl.BlockSpec(memory_space=pltpu.VMEM)
SMEM = pl.BlockSpec(memory_space=pltpu.SMEM)
ANY = pl.BlockSpec(memory_space=pl.ANY)
BF16, F32, I32 = jnp.bfloat16, jnp.float32, jnp.int32


def iota(shape, dim):
    return lax.broadcasted_iota(I32, shape, dim)


def call(body, out, n_in, specs=None, out_specs=None, cost=(0, 0), scratch=(), name=None, vmem=20):
    return pl.pallas_call(
        body,
        out_shape=out,
        in_specs=specs or [VMEM] * n_in,
        out_specs=out_specs or jax.tree.map(lambda _: VMEM, out),
        scratch_shapes=scratch,
        name=name,
        compiler_params=pltpu.CompilerParams(vmem_limit_bytes=vmem << 20),
        cost_estimate=pl.CostEstimate(flops=cost[0], bytes_accessed=cost[1], transcendentals=0),
    )


def split_ids(ids, rows_own, places):
    owner = ids // rows_own
    return owner % places, ids + (owner // places - owner) * rows_own


def slots_of_row(ids, rows_own, places, per_place):
    tokens = ids.shape[1]
    place, local = split_ids(ids, rows_own, places)
    hits = iota((places, tokens), 0) == place
    earlier = (iota((tokens, tokens), 0) < iota((tokens, tokens), 1)).astype(BF16)
    before = jnp.dot(hits.astype(BF16), earlier, preferred_element_type=F32)
    rank = jnp.sum(jnp.where(hits, before, 0.0), axis=0, keepdims=True).astype(I32)
    return place * per_place + rank, local


def pack_body(places, rows_own, token_ref, next_ref, grad_ref, out_ref, slot_ref):
    tokens, width = grad_ref.shape
    rows = out_ref.shape[0]
    step = pl.program_id(0)

    @pl.when(step == 0)
    def _():
        for lane, ids_ref in enumerate((token_ref, next_ref)):
            slot, local = slots_of_row(ids_ref[...], rows_own, places, 2 * tokens // places)
            slot_ref[2 * lane : 2 * lane + 1] = slot
            slot_ref[2 * lane + 1 : 2 * lane + 2] = local

    tags = jnp.zeros((rows, LANES), F32)
    for lane in range(2):
        slot, local = slot_ref[2 * lane : 2 * lane + 1], slot_ref[2 * lane + 1 : 2 * lane + 2]
        chosen = (iota((rows, tokens), 0) + step * rows == slot).astype(BF16)
        if lane == 0:
            out_ref[:, :width] = jnp.dot(chosen, grad_ref[...], preferred_element_type=F32).astype(BF16)
        marks = jnp.where(iota((LANES, tokens), 0) == lane, local + 1, 0).astype(F32).astype(BF16)
        tags += lax.dot_general(chosen, marks, (((1,), (1,)), ((), ())), preferred_element_type=F32)
    out_ref[:, width:] = tags.astype(BF16)


def pack(places, rows_own, token_ids, next_ids, embed_grad, pieces=4):
    tokens, width = embed_grad.shape
    slots, total = 2 * tokens, width + LANES
    whole = lambda shape: pl.BlockSpec(shape, lambda i: (0, 0))
    return pl.pallas_call(
        functools.partial(pack_body, places, rows_own),
        grid=(pieces,),
        out_shape=jax.ShapeDtypeStruct((slots, total), BF16),
        in_specs=[whole((1, tokens)), whole((1, tokens)), whole((tokens, width))],
        out_specs=pl.BlockSpec((slots // pieces, total), lambda i: (i, 0)),
        scratch_shapes=[pltpu.VMEM((8, tokens), I32)],
        name="pack",
        compiler_params=pltpu.CompilerParams(vmem_limit_bytes=60 << 20),
        cost_estimate=pl.CostEstimate(flops=2 * slots * tokens * width, bytes_accessed=4 << 20, transcendentals=0),
    )(token_ids.reshape(1, -1), next_ids.reshape(1, -1), embed_grad)


def chosen_rows(got_ref, lane, width, rows, half_ref):
    tag = got_ref[:, width + lane : width + lane + 1].astype(F32).astype(I32) - 1
    row = iota((got_ref.shape[0], rows), 1)
    half = rows // 2
    mine_first = jnp.where(row < half, row + half_ref[0] * half, row - half_ref[0] * half)
    return (tag == mine_first).astype(F32).astype(BF16)


def sum_body(half_ref, got_ref, mine_ref, other_ref):
    half, width = mine_ref.shape
    chosen = chosen_rows(got_ref, 0, width, 2 * half, half_ref)
    total = lax.dot_general(
        chosen, got_ref[:, :width], (((0,), (0,)), ((), ())), preferred_element_type=F32
    )
    mine_ref[...] = total[:half]
    other_ref[...] = total[half:]


def ask_body(half_ref, got_ref, out_ref):
    out_ref[...] = chosen_rows(got_ref, 1, got_ref.shape[1] - LANES, out_ref.shape[1], half_ref)


def adam_body(param_ref, one_ref, two_ref, proj_ref, mine_ref, other_ref, p_ref, o_ref, t_ref, table_ref):
    grad = proj_ref[...] + (mine_ref[...] + other_ref[...])
    one = 0.9 * one_ref[...] + 0.1 * grad
    two = 0.999 * two_ref[...] + 0.001 * grad * grad
    first_fix = 1.0 - 0.9**STEP
    second_fix = 1.0 - 0.999**STEP
    param = param_ref[...] - 0.01 * (one / first_fix) / (jnp.sqrt(two / second_fix) + 1e-08)
    o_ref[...] = one
    t_ref[...] = two
    p_ref[...] = param
    table_ref[...] = param.astype(BF16)


def find_body(chosen_ref, mine_ref, other_ref, out_ref):
    half = mine_ref.shape[0]
    found = jnp.dot(chosen_ref[:, :half], mine_ref[...], preferred_element_type=F32)
    found += jnp.dot(chosen_ref[:, half:], other_ref[...], preferred_element_type=F32)
    out_ref[...] = found.astype(BF16)


def route_body(places, rows_own, ids_ref, out_ref):
    tokens, slots = out_ref.shape
    place, _ = split_ids(ids_ref[...], rows_own, places)
    hits = iota((tokens, LANES), 1) == place
    earlier = (iota((tokens, tokens), 1) < iota((tokens, tokens), 0)).astype(BF16)
    before = jnp.dot(earlier, hits.astype(BF16), preferred_element_type=F32)
    rank = jnp.sum(jnp.where(hits, before, 0.0), axis=1, keepdims=True).astype(I32)
    slot = place * (slots // places) + rank
    out_ref[...] = (iota((tokens, slots), 1) == slot).astype(BF16)


def pick_body(route_ref, replies_ref, out_ref):
    out_ref[...] = jnp.dot(route_ref[...], replies_ref[...], preferred_element_type=F32).astype(BF16)


def join_body(ranks, me_ref, own_ref, up_ref, down_ref, up2_ref, down2_ref, far_ref, out_ref, sems):
    me = me_ref[0]
    last = ranks - 1
    width = own_ref.shape[1]
    plan = (
        (own_ref, me, None),
        (up_ref, me - 1, me >= 1),
        (down_ref, me + 1, me < last),
        (up2_ref, me - 2, me >= 2),
        (down2_ref, me + 2, me < last - 1),
        (far_ref, last - me, (me == 0) | (me == last)),
    )
    copies = []
    for i, (src, rank, cond) in enumerate(plan):
        start = pl.multiple_of(jnp.clip(rank, 0, last) * width, LANES)
        copies.append((cond, pltpu.make_async_copy(src, out_ref.at[:, pl.ds(start, width)], sems.at[i])))
    for method in ("start", "wait"):
        for cond, c in copies:
            if cond is None:
                getattr(c, method)()
            else:
                pl.when(cond)(getattr(c, method))


def on_device(param, moment_one, moment_two, proj_grad, embed_grad, token_ids, next_ids):
    rows_own, width = param.shape
    places = lax.axis_size(PLANE)
    ranks = lax.axis_size("tp")
    tokens = token_ids.shape[0]
    slots = 2 * tokens
    sds = jax.ShapeDtypeStruct
    half = lax.axis_index("zh").reshape(1)
    me = lax.axis_index("tp").reshape(1)

    packed = pack(places, rows_own, token_ids, next_ids, embed_grad)
    got = lax.all_to_all(
        packed.reshape(places, slots // places, width + LANES), PLANE, split_axis=0, concat_axis=0, tiled=True
    ).reshape(slots, width + LANES)
    route = call(
        functools.partial(route_body, places, rows_own), sds((tokens, slots), BF16), 1,
        cost=(2 * tokens * tokens * LANES, 2 << 20), name="route",
    )(next_ids.reshape(-1, 1))
    mine, other = call(
        sum_body, (sds((rows_own, width), F32),) * 2, 2, specs=[SMEM, VMEM],
        cost=(4 * slots * rows_own * width, 3 << 20), name="sum",
    )(half, got)
    theirs = lax.ppermute(other, "zh", PAIR)
    chosen = call(
        ask_body, sds((slots, 2 * rows_own), BF16), 2, specs=[SMEM, VMEM],
        cost=(slots * LANES, 1 << 20), name="ask",
    )(half, got)
    block = sds((rows_own, width), F32)
    new_param, new_one, new_two, table = call(
        adam_body, (block, block, block, sds((rows_own, width), BF16)), 6,
        cost=(20 * rows_own * width, 2 << 20), name="adam",
    )(param, moment_one, moment_two, proj_grad, mine, theirs)

    def reply(table, table_other):
        found = call(
            find_body, sds((slots, width), BF16), 3, cost=(4 * slots * rows_own * width, 3 << 20), name="find",
        )(chosen, table, table_other)
        return lax.all_to_all(
            found.reshape(places, slots // places, width), PLANE, split_axis=0, concat_axis=0, tiled=True
        ).reshape(slots, width)

    def pick(replies):
        return call(
            pick_body, sds((tokens, width), BF16), 2, cost=(2 * slots * tokens * width, 4 << 20), name="pick",
        )(route, replies)

    replies = reply(table, lax.ppermute(table, "zh", PAIR))
    last = ranks - 1
    far = lax.ppermute(table, "tp", [(0, last), (last, 0)])
    far_other = lax.ppermute(
        table, ("zh", "tp"), [(last, ranks), (ranks, last), (ranks + last, 0), (0, ranks + last)]
    )
    far_replies = reply(far, far_other)
    own = pick(replies)
    steps = range(ranks)
    up = lax.ppermute(own, "tp", [(i, i + 1) for i in steps[:-1]])
    down = lax.ppermute(own, "tp", [(i, i - 1) for i in steps[1:]])
    up2 = lax.ppermute(up, "tp", [(i, i + 1) for i in steps[1:-1]])
    down2 = lax.ppermute(down, "tp", [(i, i - 1) for i in steps[1:-1]])
    next_rows = call(
        functools.partial(join_body, ranks), sds((tokens, ranks * width), BF16), 0,
        specs=[SMEM] + [VMEM] * 6, out_specs=ANY, scratch=[pltpu.SemaphoreType.DMA((6,))],
        cost=(0, 8 << 20), name="join",
    )(me, own, up, down, up2, down2, pick(far_replies))
    return (new_param, new_one, new_two, next_rows)


def solution(mesh):
    grid = Mesh(mesh.devices.reshape(2, 4, 4, 2, mesh.shape["tp"]), SECTION + ("tp",))
    block = P(SECTION, "tp")
    return jax.shard_map(
        on_device,
        mesh=grid,
        in_specs=(block,) * 5 + (P(SECTION),) * 2,
        out_specs=(block,) * 3 + (P(SECTION, None),),
        check_vma=False,
    )
```

```python
import functools

import jax
import jax.numpy as jnp
from jax import lax
from jax.experimental import pallas as pl
from jax.experimental.pallas import tpu as pltpu
from jax.sharding import Mesh, PartitionSpec as P

STEP = 1000
PLANE = ("y", "x", "c")
SECTION = ("zh",) + PLANE
PAIR = [(0, 1), (1, 0)]
LANES = 128
CHUNKS = (512, 384)
VMEM = pl.BlockSpec(memory_space=pltpu.VMEM)
SMEM = pl.BlockSpec(memory_space=pltpu.SMEM)
ANY = pl.BlockSpec(memory_space=pl.ANY)
BF16, F32, I32 = jnp.bfloat16, jnp.float32, jnp.int32
sds = jax.ShapeDtypeStruct


def iota(shape, dim):
    return lax.broadcasted_iota(I32, shape, dim)


def dot(a, b, dims=((1,), (0,))):
    return lax.dot_general(a, b, (dims, ((), ())), preferred_element_type=F32)


def params(vmem):
    return pltpu.CompilerParams(vmem_limit_bytes=vmem << 20)


def cost(flops, bytes_accessed):
    return pl.CostEstimate(flops=flops, bytes_accessed=bytes_accessed, transcendentals=0)


def call(body, out, specs, flops=0, moved=1 << 20, vmem=20, **more):
    return pl.pallas_call(
        body,
        out_shape=out,
        in_specs=specs,
        out_specs=more.pop("out_specs", jax.tree.map(lambda _: VMEM, out)),
        compiler_params=params(vmem),
        cost_estimate=cost(flops, moved),
        **more,
    )


def owner_slots(ids, half, rows_own, places, cap):
    tokens = ids.shape[1]
    owner = ids // rows_own
    hits = iota((2 * places, tokens), 0) == owner
    earlier = (iota((tokens, tokens), 0) < iota((tokens, tokens), 1)).astype(BF16)
    before = dot(hits.astype(BF16), earlier)
    rank = jnp.sum(jnp.where(hits, before, 0.0), axis=0, keepdims=True).astype(I32)
    slot = (owner % places) * cap + rank
    return slot, (owner // places != half).astype(I32), ids - owner * rows_own


def pack_body(group, places, rows_own, half_ref, token_ref, next_ref, grad_ref, out_ref, slot_ref):
    tokens, width = grad_ref.shape
    rows = out_ref.shape[0]
    step = pl.program_id(0)

    @pl.when(step == 0)
    def _():
        for i, ids_ref in enumerate((token_ref, next_ref)[: 1 + group]):
            slot, theirs, local = owner_slots(ids_ref[...], half_ref[0], rows_own, places, tokens // places)
            slot_ref[3 * i : 3 * i + 1] = jnp.where(theirs == group, slot, -1)
            slot_ref[3 * i + 1 : 3 * i + 2] = jnp.where(theirs == group, -1, slot)
            slot_ref[3 * i + 2 : 3 * i + 3] = local

    row = iota((rows, tokens), 0) + step * rows
    mine = (row == slot_ref[0:1]).astype(BF16)
    out_ref[:, :width] = dot(mine, grad_ref[...]).astype(BF16)
    if group:
        tags = jnp.zeros((rows, LANES), F32)
        for lane in range(4):
            at = 3 * (lane % 2)
            hits = mine if lane == 0 else (row == slot_ref[at + lane // 2 : at + lane // 2 + 1]).astype(BF16)
            marks = jnp.where(iota((LANES, tokens), 0) == lane, slot_ref[at + 2 : at + 3] + 1, 0)
            tags += dot(hits, marks.astype(F32).astype(BF16), ((1,), (1,)))
        out_ref[:, width:] = tags.astype(BF16)


def pack(group, places, rows_own, half, token_ids, next_ids, embed_grad, pieces=2):
    tokens, width = embed_grad.shape
    total = width + LANES * group
    whole = lambda shape: pl.BlockSpec(shape, lambda i: (0, 0))
    return pl.pallas_call(
        functools.partial(pack_body, group, places, rows_own),
        grid=(pieces,),
        out_shape=sds((tokens, total), BF16),
        in_specs=[SMEM, whole((1, tokens)), whole((1, tokens)), whole((tokens, width))],
        out_specs=pl.BlockSpec((tokens // pieces, total), lambda i: (i, 0)),
        scratch_shapes=[pltpu.VMEM((8, tokens), I32)],
        name="pack",
        compiler_params=params(60),
        cost_estimate=cost(2 * tokens * tokens * width, 3 << 20),
    )(half, token_ids.reshape(1, -1), next_ids.reshape(1, -1), embed_grad)


def chosen_rows(got_ref, lane, width, rows):
    tag = got_ref[:, width + lane : width + lane + 1].astype(F32).astype(I32) - 1
    return (tag == iota((got_ref.shape[0], rows), 1)).astype(F32).astype(BF16)


def sum_body(got_ref, out_ref):
    rows, width = out_ref.shape
    out_ref[...] = dot(chosen_rows(got_ref, 0, width, rows), got_ref[:, :width], ((0,), (0,)))


def tags_body(got_ref, *out_refs):
    for lane, ref in zip((1, 3), out_refs):
        ref[...] = chosen_rows(got_ref, lane, got_ref.shape[1] - LANES, ref.shape[1])


def adam_body(param_ref, one_ref, two_ref, proj_ref, tags_ref, got_ref, other_ref, p_ref, o_ref, t_ref, *table_refs):
    rows, width = param_ref.shape
    mine = dot(chosen_rows(tags_ref, 2, width, rows), got_ref[...], ((0,), (0,)))
    grad = proj_ref[...] + (mine + other_ref[...])
    one = 0.9 * one_ref[...] + 0.1 * grad
    two = 0.999 * two_ref[...] + 0.001 * grad * grad
    first_fix = 1.0 - 0.9**STEP
    second_fix = 1.0 - 0.999**STEP
    param = param_ref[...] - 0.01 * (one / first_fix) / (jnp.sqrt(two / second_fix) + 1e-08)
    o_ref[...] = one
    t_ref[...] = two
    p_ref[...] = param
    table = param.astype(BF16)
    at = 0
    for ref in table_refs[1:]:
        ref[...] = table[:, at : at + ref.shape[1]]
        at += ref.shape[1]
    table_refs[0][...] = table


def find_body(own_ask_ref, other_ask_ref, own_ref, other_ref, out_ref):
    places, slots, width = out_ref.shape
    cap = slots // 2
    for i, (ask_ref, table_ref) in enumerate(((own_ask_ref, own_ref), (other_ask_ref, other_ref))):
        found = dot(ask_ref[...], table_ref[...]).astype(BF16)
        out_ref[:, i * cap : (i + 1) * cap, :] = found.reshape(places, cap, width)


def route_body(places, rows_own, half_ref, ids_ref, out_ref):
    tokens, slots = out_ref.shape
    owner = ids_ref[...] // rows_own
    hits = iota((tokens, LANES), 1) == owner
    earlier = (iota((tokens, tokens), 1) < iota((tokens, tokens), 0)).astype(BF16)
    before = dot(earlier, hits.astype(BF16))
    rank = jnp.sum(jnp.where(hits, before, 0.0), axis=1, keepdims=True).astype(I32)
    theirs = (owner // places != half_ref[0]).astype(I32)
    slot = (2 * (owner % places) + theirs) * (tokens // places) + rank
    out_ref[...] = (iota((tokens, slots), 1) == slot).astype(BF16)


def pick_body(route_ref, replies_ref, out_ref):
    out_ref[...] = dot(route_ref[...], replies_ref[...]).astype(BF16)


def join_body(plan, ranks, width, fresh, me_ref, *refs):
    refs = refs if fresh else refs[1:]
    n = len(plan)
    sources, out_ref, buffers, sems = refs[:n], refs[n], refs[n + 1 : -1], refs[-1]
    me = me_ref[0]
    last = ranks - 1
    where = {
        "own": (me, None),
        "up": (me - 1, me >= 1),
        "down": (me + 1, me < last),
        "up2": (me - 2, me >= 2),
        "down2": (me + 2, me < last - 1),
        "far": (last - me, (me == 0) | (me == last)),
    }
    pieces = 4

    def act(cond, method):
        method() if cond is None else pl.when(cond)(method)

    loads, stores = [], []
    for i, (kind, at) in enumerate(plan):
        rank, cond = where[kind]
        rows, size = buffers[i].shape
        rows = rows // pieces
        start = pl.multiple_of(jnp.clip(rank, 0, last) * width + at, LANES)
        for k in range(pieces):
            part = pl.ds(k * rows, rows)
            staged = buffers[i].at[part]
            loads.append((cond, pltpu.make_async_copy(sources[i].at[part], staged, sems.at[0, i, k])))
            stores.append(
                (cond, pltpu.make_async_copy(staged, out_ref.at[part, pl.ds(start, size)], sems.at[1, i, k]))
            )
    for cond, load in loads:
        act(cond, load.start)
    for (cond, load), (_, store) in zip(loads, stores):
        act(cond, load.wait)
        act(cond, store.start)
    for cond, store in stores:
        act(cond, store.wait)


def join(me, ranks, width, out, pieces):
    tokens = pieces[0][2].shape[0]
    fresh = out is None
    arrays = [p[2] for p in pieces]
    return call(
        functools.partial(join_body, [p[:2] for p in pieces], ranks, width, fresh),
        sds((tokens, ranks * width), BF16),
        [SMEM] + [ANY] * (len(pieces) + (not fresh)),
        moved=2 << 20,
        out_specs=ANY,
        scratch_shapes=[pltpu.VMEM(x.shape, BF16) for x in arrays]
        + [pltpu.SemaphoreType.DMA((2, len(pieces), 4))],
        input_output_aliases={} if fresh else {1: 0},
    )(me, *(() if fresh else (out,)), *arrays)


def on_device(param, moment_one, moment_two, proj_grad, embed_grad, token_ids, next_ids):
    rows_own, width = param.shape
    places = lax.axis_size(PLANE)
    ranks = lax.axis_size("tp")
    tokens = token_ids.shape[0]
    cap = tokens // places
    last = ranks - 1
    half = lax.axis_index("zh").reshape(1)
    me = lax.axis_index("tp").reshape(1)

    def exchange(x):
        return lax.all_to_all(x, PLANE, split_axis=0, concat_axis=0, tiled=True)

    def dispatch(group):
        packed = pack(group, places, rows_own, half, token_ids, next_ids, embed_grad)
        total = packed.shape[1]
        return exchange(packed.reshape(places, cap, total)).reshape(tokens, total)

    tagged = dispatch(1)
    theirs = call(sum_body, sds((rows_own, width), F32), [VMEM], flops=2 * tokens * rows_own * width)(tagged)
    theirs = lax.ppermute(theirs, "zh", PAIR)
    got = dispatch(0)
    route = call(
        functools.partial(route_body, places, rows_own), sds((tokens, 2 * tokens), BF16), [SMEM, VMEM],
        flops=2 * tokens * tokens * LANES,
    )(half, next_ids.reshape(-1, 1))
    block = sds((rows_own, width), F32)
    tables = tuple(sds((rows_own, n), BF16) for n in (width,) + CHUNKS)
    new_param, new_one, new_two, table, *chunks = call(
        adam_body, (block, block, block) + tables, [VMEM] * 7, flops=2 * tokens * rows_own * width,
    )(param, moment_one, moment_two, proj_grad, tagged, got, theirs)
    ask_other, ask_own = call(tags_body, (sds((tokens, rows_own), BF16),) * 2, [VMEM])(tagged)

    def reply(own, other):
        n = own.shape[1]
        found = call(
            find_body, sds((places, 2 * cap, n), BF16), [VMEM] * 4, flops=4 * tokens * rows_own * n
        )(ask_own, ask_other, own, other)
        return exchange(found).reshape(2 * tokens, n)

    def pick(replies):
        n = replies.shape[1]
        return call(pick_body, sds((tokens, n), BF16), [VMEM] * 2, flops=4 * tokens * tokens * n)(route, replies)

    others = [lax.ppermute(c, "zh", PAIR) for c in chunks]
    far = lax.ppermute(table, "tp", [(0, last), (last, 0)])
    far_other = lax.ppermute(table, ("zh", "tp"), [(last, ranks), (ranks, last), (ranks + last, 0), (0, ranks + last)])
    owns = [pick(reply(c, o)) for c, o in zip(chunks, others)]
    far_replies = reply(far, far_other)
    steps = range(ranks)
    near, next_near, at = [], [], 0
    for own in owns:
        up = lax.ppermute(own, "tp", [(i, i + 1) for i in steps[:-1]])
        down = lax.ppermute(own, "tp", [(i, i - 1) for i in steps[1:]])
        up2 = lax.ppermute(up, "tp", [(i, i + 1) for i in steps[1:-1]])
        down2 = lax.ppermute(down, "tp", [(i, i - 1) for i in steps[1:-1]])
        near.append([("own", at, own), ("up", at, up), ("down", at, down)])
        next_near.append([("up2", at, up2), ("down2", at, down2)])
        at += own.shape[1]
    far_rows = pick(far_replies)
    out = join(me, ranks, width, None, near[0] + near[1])
    out = join(me, ranks, width, out, next_near[0])
    out = join(me, ranks, width, out, [("far", 0, far_rows)])
    out = join(me, ranks, width, out, next_near[1])
    return (new_param, new_one, new_two, out)


def solution(mesh):
    grid = Mesh(mesh.devices.reshape(2, 4, 4, 2, mesh.shape["tp"]), SECTION + ("tp",))
    block = P(SECTION, "tp")
    return jax.shard_map(
        on_device,
        mesh=grid,
        in_specs=(block,) * 5 + (P(SECTION),) * 2,
        out_specs=(block,) * 3 + (P(SECTION, None),),
        check_vma=False,
    )
```

```python
import functools

import jax
import jax.numpy as jnp
from jax import lax
from jax.experimental import pallas as pl
from jax.experimental.pallas import tpu as pltpu
from jax.sharding import Mesh, PartitionSpec as P

STEP = 1000
PLANE = ("y", "x", "c")
SECTION = ("zh",) + PLANE
PAIR = [(0, 1), (1, 0)]
LANES = 128
CHUNKS = (512, 384)
VMEM = pl.BlockSpec(memory_space=pltpu.VMEM)
SMEM = pl.BlockSpec(memory_space=pltpu.SMEM)
ANY = pl.BlockSpec(memory_space=pl.ANY)
BF16, F32, I32 = jnp.bfloat16, jnp.float32, jnp.int32
sds = jax.ShapeDtypeStruct


def iota(shape, dim):
    return lax.broadcasted_iota(I32, shape, dim)


def dot(a, b, dims=((1,), (0,))):
    return lax.dot_general(a, b, (dims, ((), ())), preferred_element_type=F32)


def params(vmem):
    return pltpu.CompilerParams(vmem_limit_bytes=vmem << 20)


def cost(flops, bytes_accessed):
    return pl.CostEstimate(flops=flops, bytes_accessed=bytes_accessed, transcendentals=0)


def call(body, out, specs, flops=0, moved=1 << 20, vmem=20, **more):
    return pl.pallas_call(
        body,
        out_shape=out,
        in_specs=specs,
        out_specs=more.pop("out_specs", jax.tree.map(lambda _: VMEM, out)),
        compiler_params=params(vmem),
        cost_estimate=cost(flops, moved),
        **more,
    )


def owner_slots(ids_list, half, rows_own, places, cap):
    tokens = ids_list[0].shape[1]
    owners = [ids // rows_own for ids in ids_list]
    hits = [iota((2 * places, tokens), 0) == owner for owner in owners]
    earlier = (iota((tokens, tokens), 0) < iota((tokens, tokens), 1)).astype(BF16)
    before = dot(jnp.concatenate([h.astype(F32) for h in hits], axis=0).astype(BF16), earlier)
    found = []
    for i, (ids, owner, hit) in enumerate(zip(ids_list, owners, hits)):
        ahead = before[2 * places * i : 2 * places * (i + 1)]
        rank = jnp.sum(jnp.where(hit, ahead, 0.0), axis=0, keepdims=True).astype(I32)
        slot = (owner % places) * cap + rank
        found.append((slot, (owner // places != half).astype(I32), ids - owner * rows_own))
    return found


def pack_body(group, places, rows_own, half_ref, token_ref, next_ref, grad_ref, out_ref, slot_ref):
    tokens, width = grad_ref.shape
    rows = out_ref.shape[0]
    step = pl.program_id(0)

    @pl.when(step == 0)
    def _():
        ids_list = [ref[...] for ref in (token_ref, next_ref)[: 1 + group]]
        found = owner_slots(ids_list, half_ref[0], rows_own, places, tokens // places)
        for i, (slot, theirs, local) in enumerate(found):
            slot_ref[3 * i : 3 * i + 1] = jnp.where(theirs == group, slot, -1)
            slot_ref[3 * i + 1 : 3 * i + 2] = jnp.where(theirs == group, -1, slot)
            slot_ref[3 * i + 2 : 3 * i + 3] = local

    row = iota((rows, tokens), 0) + step * rows
    mine = (row == slot_ref[0:1]).astype(BF16)
    out_ref[:, :width] = dot(mine, grad_ref[...]).astype(BF16)
    if group:
        tags = jnp.zeros((rows, LANES), F32)
        for lane in range(4):
            at = 3 * (lane % 2)
            hits = mine if lane == 0 else (row == slot_ref[at + lane // 2 : at + lane // 2 + 1]).astype(BF16)
            marks = jnp.where(iota((LANES, tokens), 0) == lane, slot_ref[at + 2 : at + 3] + 1, 0)
            tags += dot(hits, marks.astype(F32).astype(BF16), ((1,), (1,)))
        out_ref[:, width:] = tags.astype(BF16)


def pack(group, places, rows_own, half, token_ids, next_ids, embed_grad, pieces=1):
    tokens, width = embed_grad.shape
    total = width + LANES * group
    whole = lambda shape: pl.BlockSpec(shape, lambda i: (0, 0))
    return pl.pallas_call(
        functools.partial(pack_body, group, places, rows_own),
        grid=(pieces,),
        out_shape=sds((tokens, total), BF16),
        in_specs=[SMEM, whole((1, tokens)), whole((1, tokens)), whole((tokens, width))],
        out_specs=pl.BlockSpec((tokens // pieces, total), lambda i: (i, 0)),
        scratch_shapes=[pltpu.VMEM((8, tokens), I32)],
        name="pack",
        compiler_params=params(60),
        cost_estimate=cost(2 * tokens * tokens * width, 3 << 20),
    )(half, token_ids.reshape(1, -1), next_ids.reshape(1, -1), embed_grad)


def chosen_rows(got_ref, lane, width, rows):
    tag = got_ref[:, width + lane : width + lane + 1].astype(F32).astype(I32) - 1
    return (tag == iota((got_ref.shape[0], rows), 1)).astype(F32).astype(BF16)


def sum_body(got_ref, out_ref):
    rows, width = out_ref.shape
    out_ref[...] = dot(chosen_rows(got_ref, 0, width, rows), got_ref[:, :width], ((0,), (0,)))


def tags_body(got_ref, *out_refs):
    for lane, ref in zip((1, 3), out_refs):
        ref[...] = chosen_rows(got_ref, lane, got_ref.shape[1] - LANES, ref.shape[1])


def adam(param, one, two, proj, mine, other):
    grad = proj + (mine + other)
    one = 0.9 * one + 0.1 * grad
    two = 0.999 * two + 0.001 * grad * grad
    first_fix = 1.0 - 0.9**STEP
    second_fix = 1.0 - 0.999**STEP
    return param - 0.01 * (one / first_fix) / (jnp.sqrt(two / second_fix) + 1e-08), one, two


def table_body(param_ref, one_ref, two_ref, proj_ref, tags_ref, got_ref, other_ref, table_ref):
    rows, n = table_ref.shape
    width = param_ref.shape[1]
    mine = dot(chosen_rows(tags_ref, 2, width, rows), got_ref[:, :n], ((0,), (0,)))
    held = (ref[:, :n] for ref in (param_ref, one_ref, two_ref, proj_ref))
    table_ref[...] = adam(*held, mine, other_ref[:, :n])[0].astype(BF16)


def adam_body(param_ref, one_ref, two_ref, proj_ref, tags_ref, got_ref, other_ref, p_ref, o_ref, t_ref, *table_refs):
    rows, width = param_ref.shape
    mine = dot(chosen_rows(tags_ref, 2, width, rows), got_ref[...], ((0,), (0,)))
    held = (ref[...] for ref in (param_ref, one_ref, two_ref, proj_ref))
    param, one, two = adam(*held, mine, other_ref[...])
    o_ref[...] = one
    t_ref[...] = two
    p_ref[...] = param
    table = param.astype(BF16)
    table_refs[0][...] = table
    table_refs[1][...] = table[:, width - table_refs[1].shape[1] :]


def find_body(own_ask_ref, other_ask_ref, own_ref, other_ref, out_ref):
    places, slots, width = out_ref.shape
    cap = slots // 2
    for i, (ask_ref, table_ref) in enumerate(((own_ask_ref, own_ref), (other_ask_ref, other_ref))):
        found = dot(ask_ref[...], table_ref[...]).astype(BF16)
        out_ref[:, i * cap : (i + 1) * cap, :] = found.reshape(places, cap, width)


def route_body(places, rows_own, half_ref, ids_ref, out_ref):
    tokens, slots = out_ref.shape
    owner = ids_ref[...] // rows_own
    hits = iota((tokens, LANES), 1) == owner
    earlier = (iota((tokens, tokens), 1) < iota((tokens, tokens), 0)).astype(BF16)
    before = dot(earlier, hits.astype(BF16))
    rank = jnp.sum(jnp.where(hits, before, 0.0), axis=1, keepdims=True).astype(I32)
    theirs = (owner // places != half_ref[0]).astype(I32)
    slot = (2 * (owner % places) + theirs) * (tokens // places) + rank
    out_ref[...] = (iota((tokens, slots), 1) == slot).astype(BF16)


def pick_body(route_ref, replies_ref, out_ref):
    out_ref[...] = dot(route_ref[...], replies_ref[...]).astype(BF16)


def join_body(plan, ranks, width, fresh, me_ref, *refs):
    refs = refs if fresh else refs[1:]
    n = len(plan)
    sources, out_ref, buffers, sems = refs[:n], refs[n], refs[n + 1 : -1], refs[-1]
    me = me_ref[0]
    last = ranks - 1
    where = {
        "own": (me, None),
        "up": (me - 1, me >= 1),
        "down": (me + 1, me < last),
        "up2": (me - 2, me >= 2),
        "down2": (me + 2, me < last - 1),
        "far": (last - me, (me == 0) | (me == last)),
    }
    pieces = 4

    def act(cond, method):
        method() if cond is None else pl.when(cond)(method)

    loads, stores = [], []
    for i, (kind, at) in enumerate(plan):
        rank, cond = where[kind]
        rows, size = buffers[i].shape
        rows = rows // pieces
        start = pl.multiple_of(jnp.clip(rank, 0, last) * width + at, LANES)
        for k in range(pieces):
            part = pl.ds(k * rows, rows)
            staged = buffers[i].at[part]
            loads.append((cond, pltpu.make_async_copy(sources[i].at[part], staged, sems.at[0, i, k])))
            stores.append(
                (cond, pltpu.make_async_copy(staged, out_ref.at[part, pl.ds(start, size)], sems.at[1, i, k]))
            )
    for cond, load in loads:
        act(cond, load.start)
    for (cond, load), (_, store) in zip(loads, stores):
        act(cond, load.wait)
        act(cond, store.start)
    for cond, store in stores:
        act(cond, store.wait)


def join(me, ranks, width, out, pieces):
    tokens = pieces[0][2].shape[0]
    fresh = out is None
    arrays = [p[2] for p in pieces]
    return call(
        functools.partial(join_body, [p[:2] for p in pieces], ranks, width, fresh),
        sds((tokens, ranks * width), BF16),
        [SMEM] + [ANY] * (len(pieces) + (not fresh)),
        moved=2 << 20,
        out_specs=ANY,
        scratch_shapes=[pltpu.VMEM(x.shape, BF16) for x in arrays]
        + [pltpu.SemaphoreType.DMA((2, len(pieces), 4))],
        input_output_aliases={} if fresh else {1: 0},
    )(me, *(() if fresh else (out,)), *arrays)


def on_device(param, moment_one, moment_two, proj_grad, embed_grad, token_ids, next_ids):
    rows_own, width = param.shape
    places = lax.axis_size(PLANE)
    ranks = lax.axis_size("tp")
    tokens = token_ids.shape[0]
    cap = tokens // places
    last = ranks - 1
    half = lax.axis_index("zh").reshape(1)
    me = lax.axis_index("tp").reshape(1)

    def exchange(x):
        return lax.all_to_all(x, PLANE, split_axis=0, concat_axis=0, tiled=True)

    def dispatch(group):
        packed = pack(group, places, rows_own, half, token_ids, next_ids, embed_grad)
        total = packed.shape[1]
        return exchange(packed.reshape(places, cap, total)).reshape(tokens, total)

    tagged = dispatch(1)
    theirs = call(sum_body, sds((rows_own, width), F32), [VMEM], flops=2 * tokens * rows_own * width)(tagged)
    theirs = lax.ppermute(theirs, "zh", PAIR)
    got = dispatch(0)
    route = call(
        functools.partial(route_body, places, rows_own), sds((tokens, 2 * tokens), BF16), [SMEM, VMEM],
        flops=2 * tokens * tokens * LANES,
    )(half, next_ids.reshape(-1, 1))
    block = sds((rows_own, width), F32)
    held = (param, moment_one, moment_two, proj_grad, tagged, got, theirs)
    first = call(
        table_body, sds((rows_own, CHUNKS[0]), BF16), [VMEM] * 7, flops=2 * tokens * rows_own * CHUNKS[0]
    )(*held)
    tables = tuple(sds((rows_own, n), BF16) for n in (width, CHUNKS[1]))
    new_param, new_one, new_two, table, second = call(
        adam_body, (block, block, block) + tables, [VMEM] * 7, flops=2 * tokens * rows_own * width
    )(*held)
    chunks = (first, second)
    ask_other, ask_own = call(tags_body, (sds((tokens, rows_own), BF16),) * 2, [VMEM])(tagged)

    def reply(own, other):
        n = own.shape[1]
        found = call(
            find_body, sds((places, 2 * cap, n), BF16), [VMEM] * 4, flops=4 * tokens * rows_own * n
        )(ask_own, ask_other, own, other)
        return exchange(found).reshape(2 * tokens, n)

    def pick(replies):
        n = replies.shape[1]
        return call(pick_body, sds((tokens, n), BF16), [VMEM] * 2, flops=4 * tokens * tokens * n)(route, replies)

    others = []
    for chunk in chunks:
        others.append(lax.ppermute(chunk, "zh", PAIR))
    far = lax.ppermute(table, "tp", [(0, last), (last, 0)])
    far_other = lax.ppermute(table, ("zh", "tp"), [(last, ranks), (ranks, last), (ranks + last, 0), (0, ranks + last)])
    owns = [pick(reply(c, o)) for c, o in zip(chunks, others)]
    far_replies = reply(far, far_other)
    steps = range(ranks)
    near, next_near, at = [], [], 0
    for own in owns:
        up = lax.ppermute(own, "tp", [(i, i + 1) for i in steps[:-1]])
        down = lax.ppermute(own, "tp", [(i, i - 1) for i in steps[1:]])
        up2 = lax.ppermute(up, "tp", [(i, i + 1) for i in steps[1:-1]])
        down2 = lax.ppermute(down, "tp", [(i, i - 1) for i in steps[1:-1]])
        near.append([("own", at, own), ("up", at, up), ("down", at, down)])
        next_near.append([("up2", at, up2), ("down2", at, down2)])
        at += own.shape[1]
    far_rows = pick(far_replies)
    out = join(me, ranks, width, None, near[0] + near[1])
    out = join(me, ranks, width, out, next_near[0])
    out = join(me, ranks, width, out, next_near[1])
    out = join(me, ranks, width, out, [("far", 0, far_rows)])
    return (new_param, new_one, new_two, out)


def solution(mesh):
    grid = Mesh(mesh.devices.reshape(2, 4, 4, 2, mesh.shape["tp"]), SECTION + ("tp",))
    block = P(SECTION, "tp")
    return jax.shard_map(
        on_device,
        mesh=grid,
        in_specs=(block,) * 5 + (P(SECTION),) * 2,
        out_specs=(block,) * 3 + (P(SECTION, None),),
        check_vma=False,
    )
```
